512 devices in a mesh: walk: 32 (over z, core), chol: 16 (over y, x).
Axes of the slice: x: 4, y: 4, z: 16, core: 2. Of those that a mesh axis runs over, the one named last changes fastest.
Arguments:
- walkers: float32 [64, 512, 200], P('walk'), as said below
- cholesky: float32 [32, 512, 512], P('chol'), as said below
- fields: float32 [64, 32], P('walk', 'chol'), may hold values from -4 to 4
- weights: float32 [64], P('walk'), may hold values from 0.5 to 2
- counts: int32 [64], P('walk'), may hold values from 0 to 4, as said below
Outputs:
- routed: float32 [64, 512, 200], P('walk')
- comb_marks: float32 [64], P('walk')
The draws below stay inside these ranges and needn't reach their ends.
Inputs may be any that keep to these rules, and one draw needn't show every extreme that they name: The counts sum to 64. With end as in the reference program, the copies of walkers 2 * s to 2 * (s + 1) - 1 occupy new positions from 2 * (s - 1) to 2 * (s + 2) - 1. Some walker has 4 copies in every draw. `walkers`: for every walker the intersection matrix (its first 100 rows) differs from the identity by a matrix of spectral norm below one. `cholesky`: each vector is a symmetric matrix.
All inputs are finite; a program needn't handle non-finite values.
Results may differ from the reference program's by a relative error of at most 0.0001.
Values sent between devices are 32-bit elements; how exact they have to be, the bound alone decides.
A program may use at most 64 MiB of HBM per device.

```python
import math
import jax
import jax.numpy as jnp
from jax import lax

NORB = 512
NELEC = 100
WALK_DEV = 2
TAYLOR = 3
NEWTON = 3
NCHOL = 32
WALKERS = 64


def draw_walkers(key, part):
    key_real, key_imag = jax.random.split(key)
    shape_full = (WALKERS, NORB, NELEC)
    noise_real = jax.random.normal(key_real, shape_full, jnp.float32)
    noise_imag = jax.random.normal(key_imag, shape_full, jnp.float32)
    small_scale = 0.2 * (2.0 * NELEC) ** (-0.5)
    row_ids = jnp.arange(NORB)[:, None]
    row_scale = jnp.where(row_ids < NELEC, small_scale, 0.05)
    identity = (row_ids == jnp.arange(NELEC)[None, :]).astype(jnp.float32)
    real_part = identity[None] + row_scale[None] * noise_real
    imag_part = row_scale[None] * noise_imag
    return jnp.concatenate([real_part, imag_part], axis=-1).astype(jnp.float32)


def draw_cholesky(key, part):
    key_noise, key_diag = jax.random.split(key)
    shape_full = (NCHOL, NORB, NORB)
    noise = jax.random.normal(key_noise, shape_full, jnp.float32)
    symmetric = (noise + jnp.swapaxes(noise, 1, 2)) * 0.5 ** 0.5
    sigma = 5.0 * (NCHOL * NORB) ** (-0.5)
    diagonal = jax.random.uniform(key_diag, (NCHOL,), jnp.float32, 0.5, 1.5) * (2.5 / NELEC)
    identity = jnp.eye(NORB, dtype=jnp.float32)
    return (sigma * symmetric + diagonal[:, None, None] * identity[None]).astype(jnp.float32)


def draw_counts(key, part):
    groups = WALKERS // WALK_DEV
    half_width = WALK_DEV // 2
    key_drift, key_slots = jax.random.split(key)
    drift = jax.random.randint(key_drift, (groups + 1,), -half_width, half_width + 1)
    edges = jnp.arange(groups + 1)
    drift = jnp.where(edges == 1, -half_width, drift)
    drift = jnp.where(edges == 2, half_width, drift)
    drift = jnp.where((edges == 0) | (edges == groups), 0, drift)
    copies_total = WALK_DEV + drift[1:] - drift[:-1]
    group_keys = jax.random.split(key_slots, groups)
    shuffled = jax.vmap(lambda group_key: jax.random.permutation(group_key, 4 * WALK_DEV))(group_keys)
    group_ids = jnp.arange(groups)[:, None]
    slot_ids = jnp.arange(4 * WALK_DEV)[None, :]
    scores = jnp.where((group_ids == 1) & (slot_ids < 4), slot_ids - 4, shuffled)
    ranking = jnp.argsort(scores, axis=1, stable=True)
    slot_rank = jnp.argsort(ranking, axis=1, stable=True)
    chosen = (slot_rank < copies_total[:, None]).astype(jnp.int32)
    counts = jnp.sum(chosen.reshape(groups, WALK_DEV, 4), axis=-1)
    return counts.reshape(WALKERS).astype(jnp.int32)


def shard_levels(rng, shape, pieces, low, top_value):
    def one(axis_at, parts):
        draws = jax.random.uniform(jax.random.fold_in(jax.random.fold_in(rng, 6), axis_at), (parts,), jnp.float32, low / len(pieces), top_value / len(pieces))
        return jnp.repeat(jnp.exp(draws), shape[axis_at] // parts).reshape((-1,) + (1,) * (len(shape) - axis_at - 1))

    gain = one(*pieces[0])
    for cut in pieces[1:]:
        gain = gain * one(*cut)
    return gain


def scatter_about(own_key, dims, deviation, bound, cuts=(), kind=jnp.bfloat16):
    values = jax.random.normal(own_key, dims, jnp.float32) * deviation
    if len(cuts) > 0:
        values = shard_levels(own_key, dims, cuts, -0.22, 0.18) * values
    return jnp.clip(values, min=-bound, max=bound).astype(kind)


def setup_inputs(seed: int = 0) -> dict:
    seeds = jax.random.split(jax.random.key(seed), 6)
    return {
        "walkers": draw_walkers(jax.random.fold_in(seeds[5], 71), 0),
        "cholesky": draw_cholesky(jax.random.fold_in(seeds[5], 71), 0),
        "fields": scatter_about(seeds[2], (WALKERS, NCHOL), 1.0, 4.0, ((0, 32), (1, 16)), jnp.float32),
        "weights": jnp.clip(jnp.exp(math.log(2.0) - 1.3862944 * jax.random.uniform(seeds[3], (WALKERS,), jnp.float32) ** shard_levels(seeds[3], (WALKERS,), ((0, 32),), -0.2, 0.2)), 0.5, 2.0),
        "counts": draw_counts(jax.random.fold_in(seeds[5], 71), 0),
    }


highest = lax.Precision.HIGHEST
root_dt = 0.1


def rotate(block):
    half_width = block.shape[-1] // 2
    return jnp.concatenate([-block[..., half_width:], block[..., :half_width]], axis=-1)


def complex_product(left_real, left_imag, right_real, right_imag):
    real_part = jnp.dot(left_real, right_real, precision=highest) - jnp.dot(left_imag, right_imag, precision=highest)
    imag_part = jnp.dot(left_real, right_imag, precision=highest) + jnp.dot(left_imag, right_real, precision=highest)
    return real_part, imag_part


def intersection_inverse(over_real, over_imag):
    identity = jnp.eye(over_real.shape[0], dtype=over_real.dtype)
    inv_real = identity
    inv_imag = jnp.zeros_like(identity)
    for sweep_step in range(NEWTON):
        prod_real, prod_imag = complex_product(over_real, over_imag, inv_real, inv_imag)
        inv_real, inv_imag = complex_product(inv_real, inv_imag, 2.0 * identity - prod_real, -prod_imag)
    return inv_real, inv_imag


def propagate(walker, fields_row, cholesky):
    walk_real = walker[:, :NELEC]
    walk_imag = walker[:, NELEC:]
    inv_real, inv_imag = intersection_inverse(walk_real[:NELEC], walk_imag[:NELEC])
    theta_real, theta_imag = complex_product(walk_real, walk_imag, inv_real, inv_imag)
    top_rows = cholesky[:, :NELEC, :]
    force_real = root_dt * jnp.einsum('gak,ka->g', top_rows, theta_real, precision=highest)
    force_imag = root_dt * jnp.einsum('gak,ka->g', top_rows, theta_imag, precision=highest)
    coeff_real = root_dt * force_imag
    coeff_imag = root_dt * (fields_row - force_real)
    oper_real = jnp.tensordot(coeff_real, cholesky, axes=1, precision=highest)
    oper_imag = jnp.tensordot(coeff_imag, cholesky, axes=1, precision=highest)
    taylor_term = walker
    series = walker
    for degree in range(1, TAYLOR + 1):
        taylor_term = (jnp.dot(oper_real, taylor_term, precision=highest) + jnp.dot(oper_imag, rotate(taylor_term), precision=highest)) / degree
        series = series + taylor_term
    log_weight = jnp.sum(fields_row * force_real - 0.5 * (force_real * force_real - force_imag * force_imag))
    return series, log_weight


def reference(walkers, cholesky, fields, weights, counts):
    def per_walker(walker_pair):
        return propagate(walker_pair[0], walker_pair[1], cholesky)

    propagated, log_weight = lax.map(per_walker, (walkers, fields))
    new_weights = weights * jnp.exp(log_weight)
    running = jnp.cumsum(new_weights)
    comb_marks = WALKERS * running / running[-1]
    end_marks = jnp.cumsum(counts).astype(jnp.int32)
    position = jnp.arange(WALKERS, dtype=jnp.int32)
    source = jnp.sum((end_marks[None, :] <= position[:, None]).astype(jnp.int32), axis=1).astype(jnp.int32)
    routed = jnp.take(propagated, source, axis=0)
    return routed, comb_marks
```

```python
import functools

import jax
import jax.numpy as jnp
from jax import lax
from jax.experimental import pallas as pl
from jax.experimental.pallas import tpu as pltpu
from jax.sharding import PartitionSpec as P

F32 = jnp.float32
BF16 = jnp.bfloat16
MESH = pl.DeviceIdType.MESH
TAYLOR = 3
LANES = 128
ROOT_DT = 0.1


def split(a):
    high = a.astype(BF16)
    return high, (a - high.astype(F32)).astype(BF16)


def dot(a, b):
    return jnp.dot(a, b, preferred_element_type=F32)


def dot3(a, b):
    return dot(a[0], b[0]) + (dot(a[1], b[0]) + dot(a[0], b[1]))


def block_form(c):
    re, im = c[:, :LANES], c[:, LANES:]
    return jnp.concatenate([c, jnp.concatenate([-im, re], axis=1)], axis=0)


def kernel(
    nwalk, nchol, nelec,
    walk_hbm, chol_hbm, fields_s, weights_s, counts_s,
    out_ref, comb_s,
    wbuf, top, lrows, pall, phi, plo, msgs, q1, q2, ser, fin, near, ring,
    c_sem, l_send, l_recv, f_send, f_recv, m_send, m_recv,
    g_send, g_recv, r_send, r_recv, n_send, n_recv,
):
    w = lax.axis_index("walk")
    me = lax.axis_index("chol")
    core = lax.rem(w, 2)
    chip = lax.div(w, 2)
    nchip = nwalk // 2
    partner = w + 1 - 2 * core
    walks, norb = wbuf.shape[0], wbuf.shape[1]
    rows = norb // nchol
    depth = top.shape[1]

    def walk_id(shift):
        return {"walk": lax.rem(w + nwalk + shift, nwalk)}

    def block(owner):
        return pl.ds(pl.multiple_of(owner * rows, rows), rows)

    def remote(src, dst, send, recv, device):
        return pltpu.make_async_remote_copy(
            src_ref=src, dst_ref=dst, send_sem=send, recv_sem=recv,
            device_id=device, device_id_type=MESH,
        )

    mine = block(me)
    copy_walk = pltpu.make_async_copy(walk_hbm, wbuf, c_sem.at[0])
    copy_top = pltpu.make_async_copy(chol_hbm.at[:, pl.ds(0, depth)], top, c_sem.at[1])
    copy_own = pltpu.make_async_copy(chol_hbm.at[:, mine], lrows.at[me], c_sem.at[2])
    copy_walk.start()
    copy_top.start()
    copy_own.start()

    barrier = pltpu.get_barrier_semaphore()

    @pl.loop(1, nchol)
    def _(k):
        pl.semaphore_signal(barrier, inc=1, device_id={"chol": lax.rem(me + k, nchol)}, device_id_type=MESH)

    for shift in (1, -1, 2, -2):
        pl.semaphore_signal(barrier, inc=1, device_id=walk_id(shift), device_id_type=MESH)
    pl.semaphore_wait(barrier, nchol - 1 + 4)

    def l_copy(k, owner, target):
        return remote(chol_hbm.at[core, block(target)], lrows.at[owner, core],
                      l_send.at[k], l_recv.at[k], {"chol": target})

    def f_copy(k, owner, which):
        return remote(lrows.at[owner, which], lrows.at[owner, which],
                      f_send.at[k], f_recv.at[k], {"walk": partner})

    @pl.loop(1, nchol)
    def _(k):
        l_copy(k, me, lax.rem(me + k, nchol)).start()

    copy_walk.wait()
    pall[...] = jnp.zeros_like(pall)
    for i in range(walks):
        pall[i, :, 0:nelec] = wbuf[i, :, 0:nelec]
        pall[i, :, LANES:LANES + nelec] = wbuf[i, :, nelec:2 * nelec]
    for i in range(walks):
        high, low = split(pall[i])
        phi[i] = high
        plo[i] = low

    copy_top.wait()
    top_split = split(top[...].reshape(walks * depth, norb))
    at_row = lax.broadcasted_iota(jnp.int32, (LANES, LANES), 0)
    at_col = lax.broadcasted_iota(jnp.int32, (LANES, LANES), 1)
    unit = jnp.where((at_row == at_col) & (at_row < nelec), 1.0, 0.0).astype(F32)
    unit_row = jnp.concatenate([unit, jnp.zeros_like(unit)], axis=1)
    inside = lax.broadcasted_iota(jnp.int32, (LANES, 2 * LANES), 0) < nelec

    stage = []
    for i in range(walks):
        moment = dot3(top_split, (phi[i], plo[i]))
        err = jnp.where(inside, unit_row - pall[i, 0:LANES, :], 0.0)
        stage.append((moment, err))
    later = []
    for moment, err in stage:
        left = jnp.concatenate([err, moment], axis=0)
        prod = dot3(split(left), split(block_form(err)))
        later.append((prod[:LANES], moment + prod[LANES:]))
    for i, (err2, moment) in enumerate(later):
        left = jnp.concatenate([err2, moment], axis=0)
        prod = dot3(split(left), split(block_form(err2)))
        err4 = prod[:LANES]
        moment = moment + prod[LANES:]
        tr = (unit + err4[:, :LANES]).T[:depth]
        ti = err4[:, LANES:].T[:depth]
        log_part = jnp.zeros((1, 1), F32)
        for g in range(2):
            mr = moment[g * depth:(g + 1) * depth, :LANES]
            mi = moment[g * depth:(g + 1) * depth, LANES:]
            xr = ROOT_DT * jnp.sum(mr * tr - mi * ti, keepdims=True)
            xi = ROOT_DT * jnp.sum(mr * ti + mi * tr, keepdims=True)
            field = fields_s[i, g]
            log_part = log_part + (field * xr - 0.5 * (xr * xr - xi * xi))
            at = 2 * i + g
            msgs[me, at:at + 1, :] = jnp.broadcast_to(ROOT_DT * xi, (1, LANES))
            msgs[me, 4 + at:5 + at, :] = jnp.broadcast_to(ROOT_DT * (field - xr), (1, LANES))
        msgs[me, 8 + i:9 + i, :] = jnp.broadcast_to(log_part, (1, LANES))

    def m_copy(k, owner, target):
        return remote(msgs.at[owner], msgs.at[owner], m_send.at[k], m_recv.at[k], {"chol": target})

    @pl.loop(1, nchol)
    def _(k):
        m_copy(k, me, lax.rem(me + k, nchol)).start()

    @pl.loop(1, nchol)
    def _(k):
        owner = lax.rem(me + nchol - k, nchol)
        l_copy(k, owner, owner).wait_recv()
        f_copy(k, owner, core).start()

    @pl.loop(1, nchol)
    def _(k):
        owner = lax.rem(me + nchol - k, nchol)
        m_copy(k, owner, owner).wait_recv()

    for i in range(walks):
        log_weight = msgs[0, 8 + i:9 + i, :]
        for o in range(1, nchol):
            log_weight = log_weight + msgs[o, 8 + i:9 + i, :]
        ring[0, core, i:i + 1, :] = weights_s[i] * jnp.exp(log_weight)
        ring[0, core, 2 + i:3 + i, :] = jnp.full((1, LANES), counts_s[i].astype(F32))
    half_ring = nchip // 2

    def up_slot(d):
        return d

    def down_slot(d):
        return 0 if d == 0 else half_ring + d

    def ring_start(d):
        if d == 0:
            remote(ring.at[0, core], ring.at[0, core], r_send.at[0], r_recv.at[0], {"walk": partner}).start()
            return
        up, down = up_slot(d), down_slot(d)
        remote(ring.at[up_slot(d - 1)], ring.at[up], r_send.at[up], r_recv.at[up], walk_id(2)).start()
        if d < half_ring:
            remote(ring.at[down_slot(d - 1)], ring.at[down], r_send.at[down], r_recv.at[down], walk_id(-2)).start()

    def ring_wait(d):
        if d == 0:
            remote(ring.at[0, core], ring.at[0, core], r_send.at[0], r_recv.at[0], {"walk": partner}).wait()
            return
        up, down = up_slot(d), down_slot(d)
        remote(ring.at[up_slot(d - 1)], ring.at[up], r_send.at[up], r_recv.at[up], walk_id(2)).wait()
        if d < half_ring:
            remote(ring.at[down_slot(d - 1)], ring.at[down], r_send.at[down], r_recv.at[down], walk_id(-2)).wait()

    ring_start(0)

    @pl.loop(1, nchol)
    def _(k):
        owner = lax.rem(me + nchol - k, nchol)
        f_copy(k, owner, 1 - core).wait_recv()

    copy_own.wait()

    part = rows // 2
    pieces = []
    for h in range(2):
        sums = [jnp.zeros((part, norb), F32) for _ in range(4)]
        for o in range(nchol):
            for g in range(2):
                l = lrows[o, g, h * part:(h + 1) * part, :]
                for i in range(walks):
                    for ri in range(2):
                        at = 4 * ri + 2 * i + g
                        c = jnp.concatenate([msgs[o, at:at + 1, :]] * (norb // LANES), axis=1)
                        sums[2 * i + ri] = sums[2 * i + ri] + c * l
        pieces.append(sums)
    oper = []
    for i in range(walks):
        oper.append(split(jnp.concatenate(
            [pieces[0][2 * i], pieces[1][2 * i], pieces[0][2 * i + 1], pieces[1][2 * i + 1]], axis=0)))

    def g_copy(n, src, dst, k, target):
        return remote(src, dst, g_send.at[n, k], g_recv.at[n, k], {"chol": target})

    for n in range(1, TAYLOR + 1):
        for i in range(walks):
            if n == 1:
                q = (phi[i], plo[i])
            else:
                q = split((q1 if n == 2 else q2)[i])
            y = dot3(oper[i], q)
            low = y[rows:]
            term = (y[:rows] + jnp.concatenate([-low[:, LANES:], low[:, :LANES]], axis=1)) / n
            if n == 1:
                ser[i] = pall[i, mine, :] + term
            else:
                ser[i] = ser[i] + term
            if n < TAYLOR:
                (q1 if n == 1 else q2)[i, mine, :] = term
        if n < TAYLOR:
            q = q1 if n == 1 else q2

            @pl.loop(1, nchol)
            def _(k):
                g_copy(n, q.at[:, mine], q.at[:, mine], k, lax.rem(me + k, nchol)).start()

            for s in range(4):
                d = 4 * (n - 1) + s
                ring_wait(d)
                ring_start(d + 1)

                @pl.loop(1 + 4 * s, min(nchol, 5 + 4 * s))
                def _(k):
                    owner = block(lax.rem(me + nchol - k, nchol))
                    g_copy(n, q.at[:, owner], q.at[:, owner], k, me).wait_recv()

    for side, shift in ((0, 1), (1, -1)):
        remote(ser, near.at[side], n_send.at[side], n_recv.at[side], walk_id(shift)).start()
    ring_wait(half_ring)

    zero = jnp.zeros((1, LANES), F32)
    total, base, base_count = zero, zero, zero
    for d in range(nchip):
        if d == 0:
            earlier = [core == 1, core < 0]
        elif d <= half_ring:
            earlier = [d <= chip] * 2
        else:
            earlier = [chip + (d - half_ring) >= nchip] * 2
        for c in range(2):
            pair = ring[d, c, 0:1, :] + ring[d, c, 1:2, :]
            total = total + pair
            base = base + jnp.where(earlier[c], pair, 0.0)
            base_count = base_count + jnp.where(earlier[c], ring[d, c, 2:3, :] + ring[d, c, 3:4, :], 0.0)
    running = base
    for i in range(walks):
        running = running + ring[0, core, i:i + 1, :]
        comb_s[i] = jnp.max(nwalk * walks * running / total)

    def counts_of(when_even, when_odd, i):
        return jnp.where(core == 0, ring[when_even[0], when_even[1], 2 + i:3 + i, :],
                         ring[when_odd[0], when_odd[1], 2 + i:3 + i, :])

    own_counts = [ring[0, core, 2 + i:3 + i, :] for i in range(walks)]
    left_counts = [counts_of((1, 1), (0, 0), i) for i in range(walks)]
    right_counts = [counts_of((0, 1), (half_ring + 1, 0), i) for i in range(walks)]
    left_start = base_count - left_counts[0] - left_counts[1]
    right_start = base_count + own_counts[0] + own_counts[1]
    weights_of = []
    for start, cs, valid in (
        (base_count, own_counts, w >= 0),
        (left_start, left_counts, w > 0),
        (right_start, right_counts, w < nwalk - 1),
    ):
        for i in range(walks):
            end = start + cs[i]
            picks = []
            for m in range(walks):
                target = jnp.full((1, LANES), (w * walks + m).astype(F32))
                hit = jnp.where(start <= target, 1.0, 0.0) * jnp.where(target < end, 1.0, 0.0)
                picks.append(jnp.where(valid, hit, 0.0))
            weights_of.append(picks)
            start = end
    for side, shift in ((0, 1), (1, -1)):
        remote(ser, near.at[side], n_send.at[side], n_recv.at[side], walk_id(shift)).wait()
    for m in range(walks):
        acc = jnp.zeros((rows, 2 * LANES), F32)
        for j in range(3 * walks):
            i = j % walks
            source = ser[i] if j < walks else near[j // walks - 1, i]
            pick = weights_of[j][m]
            acc = acc + jnp.concatenate([pick, pick], axis=1) * source
        fin[m] = acc

    @pl.loop(1, nchol)
    def _(k):
        g_copy(0, fin, out_ref.at[:, mine], k, lax.rem(me + k, nchol)).start()

    put_own = pltpu.make_async_copy(fin, out_ref.at[:, mine], c_sem.at[3])
    put_own.start()

    @pl.loop(1, nchol)
    def _(k):
        owner = lax.rem(me + nchol - k, nchol)
        l_copy(k, owner, owner).wait_send()
        f_copy(k, owner, core).wait_send()
        m_copy(k, owner, owner).wait_send()
        g_copy(1, q1.at[:, mine], q1.at[:, mine], k, owner).wait_send()
        g_copy(2, q2.at[:, mine], q2.at[:, mine], k, owner).wait_send()

    @pl.loop(1, nchol)
    def _(k):
        owner = lax.rem(me + nchol - k, nchol)
        g_copy(0, fin, out_ref.at[:, block(owner)], k, owner).wait()

    put_own.wait()


def solution(mesh):
    nwalk, nchol = mesh.shape["walk"], mesh.shape["chol"]

    def on_device(walkers, cholesky, fields, weights, counts):
        walks, norb, width = walkers.shape
        nelec = width // 2
        ng = cholesky.shape[0]
        rows = norb // nchol
        depth = -(-nelec // 8) * 8
        vmem = pltpu.VMEM
        dma = pltpu.SemaphoreType.DMA
        smem = pl.BlockSpec(memory_space=pltpu.SMEM)
        hbm = pl.BlockSpec(memory_space=pl.ANY)
        padded, comb = pl.pallas_call(
            functools.partial(kernel, nwalk, nchol, nelec),
            out_shape=(
                jax.ShapeDtypeStruct((walks, norb, 2 * LANES), F32),
                jax.ShapeDtypeStruct((walks,), F32),
            ),
            in_specs=[hbm, hbm, smem, smem, smem],
            out_specs=(hbm, smem),
            scratch_shapes=[
                vmem((walks, norb, width), F32),
                vmem((ng, depth, norb), F32),
                vmem((nchol, ng, rows, norb), F32),
                vmem((walks, norb, 2 * LANES), F32),
                vmem((walks, norb, 2 * LANES), BF16),
                vmem((walks, norb, 2 * LANES), BF16),
                vmem((nchol, 16, LANES), F32),
                vmem((walks, norb, 2 * LANES), F32),
                vmem((walks, norb, 2 * LANES), F32),
                vmem((walks, rows, 2 * LANES), F32),
                vmem((walks, rows, 2 * LANES), F32),
                vmem((2, walks, rows, 2 * LANES), F32),
                vmem((nwalk // 2, 2, 8, LANES), F32),
                dma((4,)),
                dma((nchol,)), dma((nchol,)), dma((nchol,)), dma((nchol,)), dma((nchol,)), dma((nchol,)),
                dma((3, nchol)), dma((3, nchol)),
                dma((nwalk // 2,)), dma((nwalk // 2,)),
                dma((2,)), dma((2,)),
            ],
            compiler_params=pltpu.CompilerParams(collective_id=0, has_side_effects=True),
        )(walkers, cholesky, fields, weights, counts)
        routed = jnp.concatenate([padded[..., :nelec], padded[..., LANES:LANES + nelec]], axis=-1)
        return routed, comb

    in_specs = (P("walk", None, None), P("chol", None, None), P("walk", "chol"), P("walk"), P("walk"))
    return jax.shard_map(
        on_device, mesh=mesh, in_specs=in_specs, out_specs=(P("walk", None, None), P("walk")), check_vma=False
    )
```

```python
import functools

import jax
import jax.numpy as jnp
from jax import lax
from jax.experimental import pallas as pl
from jax.experimental.pallas import tpu as pltpu
from jax.sharding import PartitionSpec as P

F32 = jnp.float32
BF16 = jnp.bfloat16
MESH = pl.DeviceIdType.MESH
TAYLOR = 3
LANES = 128
ROOT_DT = 0.1


def split(a):
    high = a.astype(BF16)
    return high, (a - high.astype(F32)).astype(BF16)


def dot(a, b):
    return jnp.dot(a, b, preferred_element_type=F32)


def dot3(a, b):
    return dot(a[0], b[0]) + (dot(a[1], b[0]) + dot(a[0], b[1]))


def block_form(c):
    re, im = c[:, :LANES], c[:, LANES:]
    return jnp.concatenate([c, jnp.concatenate([-im, re], axis=1)], axis=0)


def kernel(
    nwalk, nchol, nelec,
    walk_hbm, chol_hbm, fields_s, weights_s, counts_s,
    out_ref, comb_s,
    wbuf, padt, top, lrows, pall, phi, plo, msgs, acomp, abuf, q0, q1, q2, cand, qf, ring,
    c_sem, l_send, l_recv, z_send, z_recv, f_send, f_recv, m_send, m_recv,
    a_send, a_recv, g_send, g_recv, o_send, o_recv, r_send, r_recv, n_send, n_recv,
):
    w = lax.axis_index("walk")
    me = lax.axis_index("chol")
    core = lax.rem(w, 2)
    chip = lax.div(w, 2)
    nchip = nwalk // 2
    partner = w + 1 - 2 * core
    walks, norb = wbuf.shape[0], wbuf.shape[2]
    rows = norb // nchol
    depth = top.shape[1]
    half = rows // 2
    side = 4
    gx, gy = lax.rem(me, side), lax.div(me, side)
    parity = lax.rem(chip, 2)
    band = rows * side
    mine_walker, mine_half = lax.div(gy, 2), lax.rem(gy, 2)
    first = -(-nelec // 16) * 8
    quarter = LANES // 2

    def walk_id(shift):
        return {"walk": lax.rem(w + nwalk + shift, nwalk)}

    def chip_id(shift, which):
        return {"walk": 2 * lax.rem(chip + nchip + shift, nchip) + which}

    def block(owner):
        at = lax.rem(owner, side) * side + lax.div(owner, side)
        return pl.ds(pl.multiple_of(at * rows, rows), rows)

    def at_band(bx):
        return pl.ds(pl.multiple_of(bx * band, band), band)

    def chip_at(dx, dy):
        return lax.rem(gy + side + dy, side) * side + lax.rem(gx + side + dx, side)

    def remote(src, dst, send, recv, device):
        return pltpu.make_async_remote_copy(
            src_ref=src, dst_ref=dst, send_sem=send, recv_sem=recv,
            device_id=device, device_id_type=MESH,
        )

    mine = block(me)
    copy_walk = pltpu.make_async_copy(walk_hbm, wbuf, c_sem.at[0])
    copy_top = pltpu.make_async_copy(chol_hbm.at[:, pl.ds(0, depth)], top, c_sem.at[1])
    copy_own = pltpu.make_async_copy(chol_hbm.at[:, mine], lrows.at[me], c_sem.at[2])
    copy_walk.start()
    copy_top.start()
    copy_own.start()

    barrier = pltpu.get_barrier_semaphore()

    @pl.loop(1, nchol)
    def _(k):
        pl.semaphore_signal(barrier, inc=1, device_id={"chol": lax.rem(me + k, nchol)}, device_id_type=MESH)

    greet = [{"walk": partner}]
    for shift in (1, -1):
        greet += [chip_id(shift, core), chip_id(shift, 1 - core)]
    for shift in (3, -3, 4, -4):
        greet.append(chip_id(shift, core))
    for shift in (1, -1):
        greet.append({**walk_id(shift), "chol": chip_at(0, 2)})
    for device in greet:
        pl.semaphore_signal(barrier, inc=1, device_id=device, device_id_type=MESH)
    pl.semaphore_wait(barrier, nchol - 1 + len(greet))

    def piece(owner, which, part):
        return lrows.at[owner, which, pl.ds(pl.multiple_of(part * half, 8), half)]

    def l_copy(k, owner, target):
        return remote(chol_hbm.at[core, pl.ds(pl.multiple_of(
            (lax.rem(target, side) * side + lax.div(target, side)) * rows + parity * half, 8), half)],
                      piece(owner, core, parity), l_send.at[k], l_recv.at[k], {"chol": target})

    def z_copy(k, owner, part):
        return remote(piece(owner, core, part), piece(owner, core, part), z_send.at[k], z_recv.at[k],
                      chip_id(2 * lax.rem(owner, 2) - 1, core))

    def f_copy(k, owner, which, part, slot):
        return remote(piece(owner, which, part), piece(owner, which, part),
                      f_send.at[slot, k], f_recv.at[slot, k], {"walk": partner})

    @pl.loop(1, nchol)
    def _(k):
        l_copy(k, me, lax.rem(me + k, nchol)).start()

    copy_walk.wait()
    for i in range(walks):
        padt[i, 96:LANES, :] = jnp.zeros((LANES - 96, norb), F32)
        padt[i, LANES + 96:2 * LANES, :] = jnp.zeros((LANES - 96, norb), F32)
        padt[i, 0:nelec, :] = wbuf[i, 0:nelec, :]
        padt[i, LANES:LANES + nelec, :] = wbuf[i, nelec:2 * nelec, :]
    for i in range(walks):
        pall[i] = padt[i].T
        high, low = split(pall[i])
        phi[i] = high
        plo[i] = low

    copy_top.wait()
    top_split = split(top[...].reshape(walks * depth, norb))
    at_row = lax.broadcasted_iota(jnp.int32, (LANES, LANES), 0)
    at_col = lax.broadcasted_iota(jnp.int32, (LANES, LANES), 1)
    unit = jnp.where((at_row == at_col) & (at_row < nelec), 1.0, 0.0).astype(F32)
    unit_row = jnp.concatenate([unit, jnp.zeros_like(unit)], axis=1)
    inside = lax.broadcasted_iota(jnp.int32, (LANES, 2 * LANES), 0) < nelec

    stage = []
    for i in range(walks):
        moment = dot3(top_split, (phi[i], plo[i]))
        err = jnp.where(inside, unit_row - pall[i, 0:LANES, :], 0.0)
        stage.append((moment, err))
    later = []
    for moment, err in stage:
        left = jnp.concatenate([err, moment], axis=0)
        prod = dot3(split(left), split(block_form(err)))
        later.append((prod[:LANES], moment + prod[LANES:]))
    for i, (err2, moment) in enumerate(later):
        left = jnp.concatenate([err2, moment], axis=0)
        prod = dot3(split(left), split(block_form(err2)))
        err4 = prod[:LANES]
        moment = moment + prod[LANES:]
        tr = (unit + err4[:, :LANES]).T[:depth]
        ti = err4[:, LANES:].T[:depth]
        log_part = jnp.zeros((1, 1), F32)
        for g in range(2):
            mr = moment[g * depth:(g + 1) * depth, :LANES]
            mi = moment[g * depth:(g + 1) * depth, LANES:]
            xr = ROOT_DT * jnp.sum(mr * tr - mi * ti, keepdims=True)
            xi = ROOT_DT * jnp.sum(mr * ti + mi * tr, keepdims=True)
            field = fields_s[i, g]
            log_part = log_part + (field * xr - 0.5 * (xr * xr - xi * xi))
            at = 2 * i + g
            msgs[me, at:at + 1, :] = jnp.broadcast_to(ROOT_DT * xi, (1, LANES))
            msgs[me, 4 + at:5 + at, :] = jnp.broadcast_to(ROOT_DT * (field - xr), (1, LANES))
        msgs[me, 8 + i:9 + i, :] = jnp.broadcast_to(log_part, (1, LANES))

    def m_copy(k, owner, target):
        return remote(msgs.at[owner], msgs.at[owner], m_send.at[k], m_recv.at[k], {"chol": target})

    @pl.loop(1, nchol)
    def _(k):
        m_copy(k, me, lax.rem(me + k, nchol)).start()

    @pl.loop(1, nchol)
    def _(k):
        owner = lax.rem(me + nchol - k, nchol)
        l_copy(k, owner, owner).wait_recv()
        z_copy(k, owner, parity).start()
        f_copy(k, owner, core, parity, 0).start()

    @pl.loop(1, nchol)
    def _(k):
        owner = lax.rem(me + nchol - k, nchol)
        z_copy(k, owner, 1 - parity).wait_recv()
        f_copy(k, owner, core, 1 - parity, 1).start()

    @pl.loop(1, nchol)
    def _(k):
        owner = lax.rem(me + nchol - k, nchol)
        m_copy(k, owner, owner).wait_recv()

    here = nchip // 2
    for i in range(walks):
        log_weight = msgs[0, 8 + i:9 + i, :]
        for o in range(1, nchol):
            log_weight = log_weight + msgs[o, 8 + i:9 + i, :]
        ring[here, core, i:i + 1, :] = weights_s[i] * jnp.exp(log_weight)
        ring[here, core, 2 + i:3 + i, :] = jnp.full((1, LANES), counts_s[i].astype(F32))

    def spread(stage):
        if stage == 0:
            own = ring.at[here, core]
            return [remote(own, own, r_send.at[0], r_recv.at[0], {"walk": partner})] + [
                remote(own, ring.at[here - d, core], r_send.at[j], r_recv.at[j], chip_id(d, c))
                for j, d, c in ((1, 1, core), (2, 1, 1 - core), (3, -1, core), (4, -1, 1 - core))]
        if stage == 1:
            return [remote(ring.at[here - 1:here + 2], ring.at[here - d - 1:here - d + 2],
                           r_send.at[j], r_recv.at[j], chip_id(d, core)) for j, d in ((5, 3), (6, -3))]
        return [remote(ring.at[here - 4:here], ring.at[here - 8:here - 4], r_send.at[7], r_recv.at[7], chip_id(4, core)),
                remote(ring.at[here + 1:here + 4], ring.at[here + 5:here + 8], r_send.at[8], r_recv.at[8], chip_id(-4, core))]

    def spread_start(stage):
        for copy in spread(stage):
            copy.start()

    def spread_wait(stage):
        for copy in spread(stage):
            copy.wait()

    spread_start(0)

    @pl.loop(1, nchol)
    def _(k):
        owner = lax.rem(me + nchol - k, nchol)
        f_copy(k, owner, 1 - core, parity, 0).wait_recv()
        f_copy(k, owner, 1 - core, 1 - parity, 1).wait_recv()

    copy_own.wait()

    part = rows // 2
    pieces = []
    for h in range(2):
        sums = [jnp.zeros((part, norb), F32) for _ in range(4)]
        for o in range(nchol):
            for g in range(2):
                l = lrows[o, g, h * part:(h + 1) * part, :]
                for i in range(walks):
                    for ri in range(2):
                        at = 4 * ri + 2 * i + g
                        c = jnp.concatenate([msgs[o, at:at + 1, :]] * (norb // LANES), axis=1)
                        sums[2 * i + ri] = sums[2 * i + ri] + c * l
        pieces.append(sums)
    for i in range(walks):
        for ri in range(2):
            for h in range(2):
                acomp[i, ri, h * part:(h + 1) * part, :] = pieces[h][2 * i + ri]

    def band_rows(by):
        return pl.ds(pl.multiple_of(by * rows, rows), rows)

    def a_copy(d):
        to = lax.rem(gy + d, side)
        return remote(acomp.at[lax.div(to, 2)], abuf.at[:, band_rows(gy)], a_send.at[d], a_recv.at[d],
                      {"chol": chip_at(0, d)})

    for d in (2, 1, 3):
        a_copy(d).start()
    abuf[:, band_rows(gy), :] = acomp[mine_walker]
    cols = pl.multiple_of(mine_half * first, 8)
    q0[...] = jnp.concatenate(
        [padt[mine_walker, pl.ds(cols, quarter), :], padt[mine_walker, pl.ds(LANES + cols, quarter), :]], axis=0).T
    spread_wait(0)
    spread_start(1)
    q_split = split(q0[...])
    for d in (1, 3, 2):
        a_copy(d).wait_recv()
    oper = split(abuf[...].reshape(2 * band, norb))
    minus = jnp.where(lax.broadcasted_iota(jnp.int32, (band, LANES), 1) < quarter, -1.0, 1.0).astype(F32)

    def g_copy(n, q, d):
        ref = q.at[at_band(gx)]
        return remote(ref, ref, g_send.at[n, d], g_recv.at[n, d], {"chol": chip_at(d, 0)})

    series = q0[at_band(gx), :]
    for n in range(1, TAYLOR + 1):
        prod = dot3(oper, q_split)
        term = (prod[:band] + minus * pltpu.roll(prod[band:], quarter, 1)) / n
        series = series + term
        if n < TAYLOR:
            q = q1 if n == 1 else q2
            q[at_band(gx), :] = term
            for d in (2, 1, 3):
                g_copy(n - 1, q, d).start()
            if n == 1:
                spread_wait(1)
                spread_start(2)
            for d in (1, 3, 2):
                g_copy(n - 1, q, d).wait_recv()
            q_split = split(q[...])
    cand[mine_walker] = series

    def near_copy(j):
        shift = (0, 1, 1, -1, -1)[j]
        device = {"chol": chip_at(0, 0 if j in (1, 3) else 2)}
        if shift:
            device.update(walk_id(shift))
        return remote(cand.at[mine_walker], cand.at[2 * (0, 1, 1, 2, 2)[j] + mine_walker],
                      n_send.at[j], n_recv.at[j], device)

    for j in (2, 4, 0, 1, 3):
        near_copy(j).start()
    spread_wait(2)

    zero = jnp.zeros((1, LANES), F32)
    total, base, base_count = zero, zero, zero
    for d in range(-here, here):
        if d == 0:
            earlier = [core == 1, core < 0]
        elif d < 0:
            earlier = [chip + d >= 0] * 2
        else:
            earlier = [chip + d >= nchip] * 2
        for c in range(2):
            pair = ring[here + d, c, 0:1, :] + ring[here + d, c, 1:2, :]
            total = total + pair
            base = base + jnp.where(earlier[c], pair, 0.0)
            base_count = base_count + jnp.where(
                earlier[c], ring[here + d, c, 2:3, :] + ring[here + d, c, 3:4, :], 0.0)
    running = base
    for i in range(walks):
        running = running + ring[here, core, i:i + 1, :]
        comb_s[i] = jnp.max(nwalk * walks * running / total)

    def counts_of(when_even, when_odd, i):
        return jnp.where(core == 0, ring[when_even[0], when_even[1], 2 + i:3 + i, :],
                         ring[when_odd[0], when_odd[1], 2 + i:3 + i, :])

    own_counts = [ring[here, core, 2 + i:3 + i, :] for i in range(walks)]
    left_counts = [counts_of((here - 1, 1), (here, 0), i) for i in range(walks)]
    right_counts = [counts_of((here, 1), (here + 1, 0), i) for i in range(walks)]
    left_start = base_count - left_counts[0] - left_counts[1]
    right_start = base_count + own_counts[0] + own_counts[1]
    weights_of = []
    for start, cs, valid in (
        (base_count, own_counts, w >= 0),
        (left_start, left_counts, w > 0),
        (right_start, right_counts, w < nwalk - 1),
    ):
        for i in range(walks):
            end = start + cs[i]
            target = jnp.full((1, LANES), (w * walks + mine_walker).astype(F32))
            hit = jnp.where(start <= target, 1.0, 0.0) * jnp.where(target < end, 1.0, 0.0)
            weights_of.append(jnp.where(valid, hit, 0.0))
            start = end
    def o_copy(c, sem, origin, to):
        (da, db), (ta, tb) = origin, to
        dx, dy = (da, db) if c == 0 else (db, da)
        tx, ty = (ta, tb) if c == 0 else (tb, ta)
        ref = qf.at[lax.rem(gy + side + dy, side),
                    pl.ds(pl.multiple_of(lax.rem(gx + side + dx, side) * band + c * (band // 2), band // 2), band // 2)]
        return remote(ref, ref, o_send.at[c, sem], o_recv.at[c, sem], {"chol": chip_at(tx, ty)})

    def o_send_first(c, d):
        return o_copy(c, d, (0, 0), (d, 0))

    def o_send_second(c, d, e):
        return o_copy(c, 4 * d + e, (-d, 0), (0, e)) if d else o_copy(c, 16 + e, (0, 0), (0, e))

    def o_recv_first(c, d):
        return o_copy(c, d, (-d, 0), (d, 0))

    def o_recv_second(c, d, e):
        return o_copy(c, 4 * d + e, (-d, -e), (0, e)) if d else o_copy(c, 16 + e, (0, -e), (0, e))

    for j in range(5):
        near_copy(j).wait_send()
    for j in range(5):
        shift = (0, 1, 1, -1, -1)[j]
        slot = 2 * (0, 1, 1, 2, 2)[j] + (mine_walker if j in (1, 3) else 1 - mine_walker)
        remote(cand.at[slot], cand.at[slot], n_send.at[j], n_recv.at[j], walk_id(1)).wait_recv()
    acc = jnp.zeros((band, LANES), F32)
    for j in range(3 * walks):
        acc = acc + weights_of[j] * cand[j]
    qf[gy, at_band(gx), :] = acc
    for d in (2, 1, 3):
        for c in range(2):
            o_send_first(c, d).start()
    for d in (2, 1, 3):
        for c in range(2):
            o_send_second(c, 0, d).start()
    for d in (1, 3, 2):
        for c in range(2):
            o_recv_first(c, d).wait_recv()
            for e in (2, 1, 3):
                o_send_second(c, d, e).start()
    for c in range(2):
        for d in (0, 1, 3, 2):
            for e in (1, 3, 2):
                o_recv_second(c, d, e).wait_recv()
    rest = nelec - first
    for i in range(walks):
        for h in range(2):
            turned = qf[2 * i + h].T
            size = rest if h else first
            wbuf[i, h * first:h * first + size, :] = turned[:size]
            wbuf[i, nelec + h * first:nelec + h * first + size, :] = turned[quarter:quarter + size]
        pltpu.make_async_copy(wbuf.at[i], out_ref.at[i], c_sem.at[3 + i]).start()

    @pl.loop(1, nchol)
    def _(k):
        owner = lax.rem(me + nchol - k, nchol)
        l_copy(k, owner, owner).wait_send()
        z_copy(k, owner, parity).wait_send()
        f_copy(k, owner, core, parity, 0).wait_send()
        f_copy(k, owner, core, 1 - parity, 1).wait_send()
        m_copy(k, owner, owner).wait_send()

    for d in range(1, side):
        a_copy(d).wait_send()
        g_copy(0, q1, d).wait_send()
        g_copy(1, q2, d).wait_send()
        for c in range(2):
            o_send_first(c, d).wait_send()
            for e in range(side):
                o_send_second(c, e, d).wait_send()
    for i in range(walks):
        pltpu.make_async_copy(wbuf.at[i], out_ref.at[i], c_sem.at[3 + i]).wait()


def solution(mesh):
    nwalk, nchol = mesh.shape["walk"], mesh.shape["chol"]

    def on_device(walkers, cholesky, fields, weights, counts):
        walks, norb, width = walkers.shape
        nelec = width // 2
        ng = cholesky.shape[0]
        rows = norb // nchol
        depth = -(-nelec // 8) * 8
        vmem = pltpu.VMEM
        dma = pltpu.SemaphoreType.DMA
        smem = pl.BlockSpec(memory_space=pltpu.SMEM)
        hbm = pl.BlockSpec(memory_space=pl.ANY)
        routed, comb = pl.pallas_call(
            functools.partial(kernel, nwalk, nchol, nelec),
            out_shape=(
                jax.ShapeDtypeStruct((walks, width, norb), F32),
                jax.ShapeDtypeStruct((walks,), F32),
            ),
            in_specs=[hbm, hbm, smem, smem, smem],
            out_specs=(hbm, smem),
            scratch_shapes=[
                vmem((walks, width, norb), F32),
                vmem((walks, 2 * LANES, norb), F32),
                vmem((ng, depth, norb), F32),
                vmem((nchol, ng, rows, norb), F32),
                vmem((walks, norb, 2 * LANES), F32),
                vmem((walks, norb, 2 * LANES), BF16),
                vmem((walks, norb, 2 * LANES), BF16),
                vmem((nchol, 16, LANES), F32),
                vmem((walks, 2, rows, norb), F32),
                vmem((2, 4 * rows, norb), F32),
                vmem((norb, LANES), F32),
                vmem((norb, LANES), F32),
                vmem((norb, LANES), F32),
                vmem((3 * walks, 4 * rows, LANES), F32),
                vmem((4, norb, LANES), F32),
                vmem((nwalk // 2, 2, 8, LANES), F32),
                dma((5,)),
                dma((nchol,)), dma((nchol,)), dma((nchol,)), dma((nchol,)),
                dma((2, nchol)), dma((2, nchol)), dma((nchol,)), dma((nchol,)),
                dma((4,)), dma((4,)), dma((2, 4)), dma((2, 4)), dma((2, 20)), dma((2, 20)),
                dma((9,)), dma((9,)),
                dma((5,)), dma((5,)),
            ],
            compiler_params=pltpu.CompilerParams(collective_id=0, has_side_effects=True),
        )(jnp.swapaxes(walkers, 1, 2), cholesky, fields, weights, counts)
        return jnp.swapaxes(routed, 1, 2), comb

    in_specs = (P("walk", None, None), P("chol", None, None), P("walk", "chol"), P("walk"), P("walk"))
    return jax.shard_map(
        on_device, mesh=mesh, in_specs=in_specs, out_specs=(P("walk", None, None), P("walk")), check_vma=False
    )
```

```python
import functools

import jax
import jax.numpy as jnp
from jax import lax
from jax.experimental import pallas as pl
from jax.experimental.pallas import tpu as pltpu
from jax.sharding import PartitionSpec as P

F32 = jnp.float32
BF16 = jnp.bfloat16
MESH = pl.DeviceIdType.MESH
TAYLOR = 3
LANES = 128
ROOT_DT = 0.1


def split(a):
    high = a.astype(BF16)
    return high, (a - high.astype(F32)).astype(BF16)


def dot(a, b):
    return jnp.dot(a, b, preferred_element_type=F32)


def dot3(a, b):
    return dot(a[0], b[0]) + (dot(a[1], b[0]) + dot(a[0], b[1]))


def block_form(c):
    re, im = c[:, :LANES], c[:, LANES:]
    return jnp.concatenate([c, jnp.concatenate([-im, re], axis=1)], axis=0)


def kernel(
    nwalk, nchol, nelec,
    walk_hbm, chol_hbm, fields_s, weights_s, counts_s,
    out_ref, comb_s,
    wbuf, padt, top, lrows, pall, phi, plo, msgs, acomp, abuf, q0, q1, q2, cnew, pcand, qf, ring, tally,
    c_sem, l_send, l_recv, z_send, z_recv, f_send, f_recv, m_send, m_recv,
    a_send, a_recv, s_send, s_recv, g_send, g_recv, o_send, o_recv, r_send, r_recv, t_send, t_recv, n_send, n_recv,
):
    w = lax.axis_index("walk")
    me = lax.axis_index("chol")
    core = lax.rem(w, 2)
    chip = lax.div(w, 2)
    nchip = nwalk // 2
    partner = w + 1 - 2 * core
    walks, norb = wbuf.shape[0], wbuf.shape[2]
    rows = norb // nchol
    depth = top.shape[1]
    half = rows // 2
    side = 4
    gx, gy = lax.rem(me, side), lax.div(me, side)
    parity = lax.rem(chip, 2)
    band = rows * side
    mine_walker, mine_half = lax.div(gy, 2), lax.rem(gy, 2)
    first = -(-nelec // 16) * 8
    quarter = LANES // 2

    def walk_id(shift):
        return {"walk": lax.rem(w + nwalk + shift, nwalk)}

    def chip_id(shift, which):
        return {"walk": 2 * lax.rem(chip + nchip + shift, nchip) + which}

    def block(owner):
        at = lax.rem(owner, side) * side + lax.div(owner, side)
        return pl.ds(pl.multiple_of(at * rows, rows), rows)

    def at_band(bx):
        return pl.ds(pl.multiple_of(bx * band, band), band)

    def chip_at(dx, dy):
        return lax.rem(gy + side + dy, side) * side + lax.rem(gx + side + dx, side)

    def remote(src, dst, send, recv, device):
        return pltpu.make_async_remote_copy(
            src_ref=src, dst_ref=dst, send_sem=send, recv_sem=recv,
            device_id=device, device_id_type=MESH,
        )

    mine = block(me)
    copy_walk = pltpu.make_async_copy(walk_hbm, wbuf, c_sem.at[0])
    copy_top = pltpu.make_async_copy(chol_hbm.at[:, pl.ds(0, depth)], top, c_sem.at[1])
    copy_own = pltpu.make_async_copy(chol_hbm.at[:, mine], lrows.at[me], c_sem.at[2])
    copy_walk.start()
    copy_top.start()
    copy_own.start()

    barrier = pltpu.get_barrier_semaphore()

    @pl.loop(1, nchol)
    def _(k):
        pl.semaphore_signal(barrier, inc=1, device_id={"chol": lax.rem(me + k, nchol)}, device_id_type=MESH)

    greet = [{"walk": partner}]
    for shift in (1, -1):
        greet += [chip_id(shift, core), chip_id(shift, 1 - core)]
    for shift in (3, -3, 4, -4):
        greet.append(chip_id(shift, core))
    for device in greet:
        pl.semaphore_signal(barrier, inc=1, device_id=device, device_id_type=MESH)
    pl.semaphore_wait(barrier, nchol - 1 + len(greet))

    def piece(owner, which, part):
        return lrows.at[owner, which, pl.ds(pl.multiple_of(part * half, 8), half)]

    def l_copy(k, owner, target):
        return remote(chol_hbm.at[core, pl.ds(pl.multiple_of(
            (lax.rem(target, side) * side + lax.div(target, side)) * rows + parity * half, 8), half)],
                      piece(owner, core, parity), l_send.at[k], l_recv.at[k], {"chol": target})

    def z_copy(k, owner, part):
        return remote(piece(owner, core, part), piece(owner, core, part), z_send.at[k], z_recv.at[k],
                      chip_id(2 * lax.rem(owner, 2) - 1, core))

    def f_copy(k, owner, which, part, slot):
        return remote(piece(owner, which, part), piece(owner, which, part),
                      f_send.at[slot, k], f_recv.at[slot, k], {"walk": partner})

    @pl.loop(1, nchol)
    def _(k):
        l_copy(k, me, lax.rem(me + k, nchol)).start()

    here = nchip // 2

    def spread(buf, send, recv, stage):
        if stage == 0:
            own = buf.at[here, core]
            return [remote(own, own, send.at[0], recv.at[0], {"walk": partner})] + [
                remote(own, buf.at[here - d, core], send.at[j], recv.at[j], chip_id(d, c))
                for j, d, c in ((1, 1, core), (2, 1, 1 - core), (3, -1, core), (4, -1, 1 - core))]
        if stage == 1:
            return [remote(buf.at[here - 1:here + 2], buf.at[here - d - 1:here - d + 2],
                           send.at[j], recv.at[j], chip_id(d, core)) for j, d in ((5, 3), (6, -3))]
        return [remote(buf.at[here - 4:here], buf.at[here - 8:here - 4], send.at[7], recv.at[7], chip_id(4, core)),
                remote(buf.at[here + 1:here + 4], buf.at[here + 5:here + 8], send.at[8], recv.at[8], chip_id(-4, core))]

    weights_run, counts_run = (ring, r_send, r_recv), (tally, t_send, t_recv)

    def spread_start(run, stage):
        for copy in spread(*run, stage):
            copy.start()

    def spread_wait(run, stage):
        for copy in spread(*run, stage):
            copy.wait()

    for i in range(walks):
        tally[here, core, i:i + 1, :] = jnp.full((1, LANES), counts_s[i].astype(F32))
    spread_start(counts_run, 0)

    copy_walk.wait()
    for i in range(walks):
        padt[i, :, 96:LANES, :] = jnp.zeros((2, LANES - 96, norb), F32)
        padt[i, 0, 0:nelec, :] = wbuf[i, 0:nelec, :]
        padt[i, 1, 0:nelec, :] = wbuf[i, nelec:2 * nelec, :]
    for i in range(walks):
        pall[i] = padt[i].reshape(2 * LANES, norb).T
        high, low = split(pall[i])
        phi[i] = high
        plo[i] = low

    copy_top.wait()
    top_split = split(top[...].reshape(walks * depth, norb))
    at_row = lax.broadcasted_iota(jnp.int32, (LANES, LANES), 0)
    at_col = lax.broadcasted_iota(jnp.int32, (LANES, LANES), 1)
    unit = jnp.where((at_row == at_col) & (at_row < nelec), 1.0, 0.0).astype(F32)
    unit_row = jnp.concatenate([unit, jnp.zeros_like(unit)], axis=1)
    inside = lax.broadcasted_iota(jnp.int32, (LANES, 2 * LANES), 0) < nelec

    stage = []
    for i in range(walks):
        moment = dot3(top_split, (phi[i], plo[i]))
        err = jnp.where(inside, unit_row - pall[i, 0:LANES, :], 0.0)
        stage.append((moment, err))
    later = []
    for moment, err in stage:
        left = jnp.concatenate([err, moment], axis=0)
        prod = dot3(split(left), split(block_form(err)))
        later.append((prod[:LANES], moment + prod[LANES:]))
    for i, (err2, moment) in enumerate(later):
        left = jnp.concatenate([err2, moment], axis=0)
        prod = dot3(split(left), split(block_form(err2)))
        err4 = prod[:LANES]
        moment = moment + prod[LANES:]
        tr = (unit + err4[:, :LANES]).T[:depth]
        ti = err4[:, LANES:].T[:depth]
        log_part = jnp.zeros((1, 1), F32)
        for g in range(2):
            mr = moment[g * depth:(g + 1) * depth, :LANES]
            mi = moment[g * depth:(g + 1) * depth, LANES:]
            xr = ROOT_DT * jnp.sum(mr * tr - mi * ti, keepdims=True)
            xi = ROOT_DT * jnp.sum(mr * ti + mi * tr, keepdims=True)
            field = fields_s[i, g]
            log_part = log_part + (field * xr - 0.5 * (xr * xr - xi * xi))
            at = 2 * i + g
            msgs[0, me, at:at + 1, :] = jnp.broadcast_to(ROOT_DT * xi, (1, LANES))
            msgs[0, me, 4 + at:5 + at, :] = jnp.broadcast_to(ROOT_DT * (field - xr), (1, LANES))
        msgs[0, me, 8 + i:9 + i, :] = jnp.broadcast_to(log_part, (1, LANES))

    spread_wait(counts_run, 0)
    spread_start(counts_run, 1)

    def m_copy(k, owner, target):
        return remote(msgs.at[0, owner], msgs.at[0, owner], m_send.at[k], m_recv.at[k], {"chol": target})

    @pl.loop(1, nchol)
    def _(k):
        m_copy(k, me, lax.rem(me + k, nchol)).start()

    @pl.loop(1, nchol)
    def _(k):
        owner = lax.rem(me + nchol - k, nchol)
        l_copy(k, owner, owner).wait_recv()
        z_copy(k, owner, parity).start()
        f_copy(k, owner, core, parity, 0).start()

    @pl.loop(1, nchol)
    def _(k):
        owner = lax.rem(me + nchol - k, nchol)
        m_copy(k, owner, owner).wait_recv()

    cols = pl.multiple_of(mine_half * first, 8)

    def n_copy(j, shift):
        return remote(msgs.at[0, :, pl.ds(0, 8)], msgs.at[j + 1, :, pl.ds(0, 8)], n_send.at[j], n_recv.at[j], walk_id(shift))

    def p_copy(j, shift):
        return remote(padt.at[:, :, pl.ds(cols, quarter)], pcand.at[j], n_send.at[2 + j], n_recv.at[2 + j], walk_id(shift))

    n_copy(0, 1).start()
    n_copy(1, -1).start()
    spread_wait(counts_run, 1)
    spread_start(counts_run, 2)

    @pl.loop(1, nchol)
    def _(k):
        owner = lax.rem(me + nchol - k, nchol)
        z_copy(k, owner, 1 - parity).wait_recv()
        f_copy(k, owner, core, 1 - parity, 1).start()

    p_copy(0, 1).start()
    p_copy(1, -1).start()

    for i in range(walks):
        log_weight = msgs[0, 0, 8 + i:9 + i, :]
        for o in range(1, nchol):
            log_weight = log_weight + msgs[0, o, 8 + i:9 + i, :]
        ring[here, core, i:i + 1, :] = weights_s[i] * jnp.exp(log_weight)

    spread_start(weights_run, 0)

    @pl.loop(1, nchol)
    def _(k):
        owner = lax.rem(me + nchol - k, nchol)
        f_copy(k, owner, 1 - core, parity, 0).wait_recv()
        f_copy(k, owner, 1 - core, 1 - parity, 1).wait_recv()

    spread_wait(counts_run, 2)
    zero = jnp.zeros((1, LANES), F32)
    base_count = zero
    for d in range(-here, here):
        if d == 0:
            earlier = [core == 1, core < 0]
        elif d < 0:
            earlier = [chip + d >= 0] * 2
        else:
            earlier = [chip + d >= nchip] * 2
        for c in range(2):
            base_count = base_count + jnp.where(
                earlier[c], tally[here + d, c, 0:1, :] + tally[here + d, c, 1:2, :], 0.0)
    def counts_of(when_even, when_odd, i):
        return jnp.where(core == 0, tally[when_even[0], when_even[1], i:i + 1, :],
                         tally[when_odd[0], when_odd[1], i:i + 1, :])

    own_counts = [tally[here, core, i:i + 1, :] for i in range(walks)]
    left_counts = [counts_of((here - 1, 1), (here, 0), i) for i in range(walks)]
    right_counts = [counts_of((here, 1), (here + 1, 0), i) for i in range(walks)]
    left_start = base_count - left_counts[0] - left_counts[1]
    right_start = base_count + own_counts[0] + own_counts[1]
    weights_of = []
    for start, cs, valid in (
        (base_count, own_counts, w >= 0),
        (left_start, left_counts, w > 0),
        (right_start, right_counts, w < nwalk - 1),
    ):
        for i in range(walks):
            end = start + cs[i]
            picks = []
            for m in range(walks):
                target = jnp.full((1, LANES), (w * walks + m).astype(F32))
                hit = jnp.where(start <= target, 1.0, 0.0) * jnp.where(target < end, 1.0, 0.0)
                picks.append(jnp.where(valid, hit, 0.0))
            weights_of.append(picks)
            start = end
    n_copy(0, 1).wait_recv()
    n_copy(1, -1).wait_recv()
    for ri in range(2):
        for m in range(walks):
            for g in range(2):
                acc = jnp.zeros((nchol, LANES), F32)
                for j in range(3 * walks):
                    acc = acc + weights_of[j][m] * msgs[j // walks, :, 4 * ri + 2 * (j % walks) + g, :]
                cnew[4 * ri + 2 * m + g] = acc

    copy_own.wait()

    part = rows // 2
    pieces = []
    for h in range(2):
        sums = [jnp.zeros((part, norb), F32) for _ in range(4)]
        for o in range(nchol):
            for g in range(2):
                l = lrows[o, g, h * part:(h + 1) * part, :]
                for i in range(walks):
                    for ri in range(2):
                        at = 4 * ri + 2 * i + g
                        c = jnp.concatenate([cnew[at, o:o + 1, :]] * (norb // LANES), axis=1)
                        sums[2 * i + ri] = sums[2 * i + ri] + c * l
        pieces.append(sums)
    for i in range(walks):
        for ri in range(2):
            for h in range(2):
                acomp[i, ri, h * part:(h + 1) * part, :] = pieces[h][2 * i + ri]

    def band_rows(by):
        return pl.ds(pl.multiple_of(by * rows, rows), rows)

    def a_copy(d):
        to = lax.rem(gy + d, side)
        return remote(acomp.at[lax.div(to, 2)], abuf.at[:, band_rows(gy)], a_send.at[d], a_recv.at[d],
                      {"chol": chip_at(0, d)})

    for d in (2, 1, 3):
        a_copy(d).start()
    abuf[:, band_rows(gy), :] = acomp[mine_walker]
    p_copy(0, 1).wait_recv()
    p_copy(1, -1).wait_recv()
    picked = jnp.zeros((2, quarter, norb), F32)
    for j in range(3 * walks):
        i = j % walks
        source = padt[i, :, pl.ds(cols, quarter), :] if j < walks else pcand[j // walks - 1, i]
        pick = jnp.where(mine_walker == 0, weights_of[j][0], weights_of[j][1])
        picked = picked + jnp.concatenate([pick] * (norb // LANES), axis=1)[None] * source
    q0[...] = picked.reshape(2 * quarter, norb).T
    spread_wait(weights_run, 0)
    spread_start(weights_run, 1)
    q_split = split(q0[...])
    minus = jnp.where(lax.broadcasted_iota(jnp.int32, (band, LANES), 1) < quarter, -1.0, 1.0).astype(F32)

    def apply(oper, values, depth_of):
        prod = dot3(oper, values)
        return prod[:depth_of] + minus[:depth_of] * pltpu.roll(prod[depth_of:], quarter, 1)

    def strip(by):
        return pl.ds(pl.multiple_of(gx * band + by * rows, rows), rows)

    def s_copy(e, d):
        ref = q1.at[strip(lax.rem(gy + side - e, side))]
        return remote(ref, ref, s_send.at[e, d], s_recv.at[e, d], {"chol": chip_at(d, 0)})

    for e in (0, 1, 3, 2):
        by = lax.rem(gy + side - e, side)
        if e:
            a_copy(e).wait_recv()
        q1[strip(by), :] = apply(split(abuf[:, band_rows(by), :].reshape(2 * rows, norb)), q_split, rows)
        for d in (2, 1, 3):
            s_copy(e, d).start()
    oper = split(abuf[...].reshape(2 * band, norb))

    def g_copy(n, q, d):
        ref = q.at[at_band(gx)]
        return remote(ref, ref, g_send.at[n, d], g_recv.at[n, d], {"chol": chip_at(d, 0)})

    series = q0[at_band(gx), :] + q1[at_band(gx), :]
    spread_wait(weights_run, 1)
    spread_start(weights_run, 2)
    for n in range(2, TAYLOR + 1):
        if n == 2:
            for e in (0, 1, 3, 2):
                for d in (1, 3, 2):
                    s_copy(e, d).wait_recv()
            term = apply(oper, split(q1[...]), band) / n
            q2[at_band(gx), :] = term
            for d in (2, 1, 3):
                g_copy(1, q2, d).start()
        else:
            for d in (1, 3, 2):
                g_copy(1, q2, d).wait_recv()
            term = apply(oper, split(q2[...]), band) / n
        series = series + term
    turned = series.T
    for c in range(2):
        qf[gy, c, :, at_band(gx)] = turned[c * quarter:c * quarter + first]

    def o_copy(c, sem, origin, to):
        (da, db), (ta, tb) = origin, to
        dx, dy = (da, db) if c == 0 else (db, da)
        tx, ty = (ta, tb) if c == 0 else (tb, ta)
        ref = qf.at[lax.rem(gy + side + dy, side), c, :,
                    pl.ds(pl.multiple_of(lax.rem(gx + side + dx, side) * band, band), band)]
        return remote(ref, ref, o_send.at[c, sem], o_recv.at[c, sem], {"chol": chip_at(tx, ty)})

    def o_send_first(c, d):
        return o_copy(c, d, (0, 0), (d, 0))

    def o_send_second(c, d, e):
        return o_copy(c, 4 * d + e, (-d, 0), (0, e)) if d else o_copy(c, 16 + e, (0, 0), (0, e))

    def o_recv_first(c, d):
        return o_copy(c, d, (-d, 0), (d, 0))

    def o_recv_second(c, d, e):
        return o_copy(c, 4 * d + e, (-d, -e), (0, e)) if d else o_copy(c, 16 + e, (0, -e), (0, e))

    for d in (2, 1, 3):
        for c in range(2):
            o_send_first(c, d).start()
    for d in (2, 1, 3):
        for c in range(2):
            o_send_second(c, 0, d).start()
    spread_wait(weights_run, 2)
    zero = jnp.zeros((1, LANES), F32)
    total, base = zero, zero
    for d in range(-here, here):
        if d == 0:
            earlier = [core == 1, core < 0]
        elif d < 0:
            earlier = [chip + d >= 0] * 2
        else:
            earlier = [chip + d >= nchip] * 2
        for c in range(2):
            pair = ring[here + d, c, 0:1, :] + ring[here + d, c, 1:2, :]
            total = total + pair
            base = base + jnp.where(earlier[c], pair, 0.0)
    running = base
    for i in range(walks):
        running = running + ring[here, core, i:i + 1, :]
        comb_s[i] = jnp.max(nwalk * walks * running / total)

    for d in (1, 3, 2):
        for c in range(2):
            o_recv_first(c, d).wait_recv()
            for e in (2, 1, 3):
                o_send_second(c, d, e).start()
    for c in range(2):
        for d in (0, 1, 3, 2):
            for e in (1, 3, 2):
                o_recv_second(c, d, e).wait_recv()
    rest = nelec - first
    for i in range(walks):
        for c in range(2):
            wbuf[i, c * nelec:c * nelec + first, :] = qf[2 * i, c]
            wbuf[i, c * nelec + first:(c + 1) * nelec, :] = qf[2 * i + 1, c, 0:rest, :]
        pltpu.make_async_copy(wbuf.at[i], out_ref.at[i], c_sem.at[3 + i]).start()

    @pl.loop(1, nchol)
    def _(k):
        owner = lax.rem(me + nchol - k, nchol)
        l_copy(k, owner, owner).wait_send()
        z_copy(k, owner, parity).wait_send()
        f_copy(k, owner, core, parity, 0).wait_send()
        f_copy(k, owner, core, 1 - parity, 1).wait_send()
        m_copy(k, owner, owner).wait_send()

    for copy in (n_copy, p_copy):
        copy(0, 1).wait_send()
        copy(1, -1).wait_send()
    for d in range(1, side):
        a_copy(d).wait_send()
        for e in range(side):
            s_copy(e, d).wait_send()
        g_copy(1, q2, d).wait_send()
        for c in range(2):
            o_send_first(c, d).wait_send()
            for e in range(side):
                o_send_second(c, e, d).wait_send()
    for i in range(walks):
        pltpu.make_async_copy(wbuf.at[i], out_ref.at[i], c_sem.at[3 + i]).wait()


def solution(mesh):
    nwalk, nchol = mesh.shape["walk"], mesh.shape["chol"]

    def on_device(walkers, cholesky, fields, weights, counts):
        walks, norb, width = walkers.shape
        nelec = width // 2
        ng = cholesky.shape[0]
        rows = norb // nchol
        depth = -(-nelec // 8) * 8
        vmem = pltpu.VMEM
        dma = pltpu.SemaphoreType.DMA
        smem = pl.BlockSpec(memory_space=pltpu.SMEM)
        hbm = pl.BlockSpec(memory_space=pl.ANY)
        routed, comb = pl.pallas_call(
            functools.partial(kernel, nwalk, nchol, nelec),
            out_shape=(
                jax.ShapeDtypeStruct((walks, width, norb), F32),
                jax.ShapeDtypeStruct((walks,), F32),
            ),
            in_specs=[hbm, hbm, smem, smem, smem],
            out_specs=(hbm, smem),
            scratch_shapes=[
                vmem((walks, width, norb), F32),
                vmem((walks, 2, LANES, norb), F32),
                vmem((ng, depth, norb), F32),
                vmem((nchol, ng, rows, norb), F32),
                vmem((walks, norb, 2 * LANES), F32),
                vmem((walks, norb, 2 * LANES), BF16),
                vmem((walks, norb, 2 * LANES), BF16),
                vmem((3, nchol, 16, LANES), F32),
                vmem((walks, 2, rows, norb), F32),
                vmem((2, 4 * rows, norb), F32),
                vmem((norb, LANES), F32),
                vmem((norb, LANES), F32),
                vmem((norb, LANES), F32),
                vmem((8, nchol, LANES), F32),
                vmem((2, walks, 2, LANES // 2, norb), F32),
                vmem((4, 2, -(-nelec // 16) * 8, norb), F32),
                vmem((nwalk // 2, 2, 8, LANES), F32),
                vmem((nwalk // 2, 2, 8, LANES), F32),
                dma((5,)),
                dma((nchol,)), dma((nchol,)), dma((nchol,)), dma((nchol,)),
                dma((2, nchol)), dma((2, nchol)), dma((nchol,)), dma((nchol,)),
                dma((4,)), dma((4,)), dma((4, 4)), dma((4, 4)), dma((2, 4)), dma((2, 4)), dma((2, 20)), dma((2, 20)),
                dma((9,)), dma((9,)), dma((9,)), dma((9,)),
                dma((4,)), dma((4,)),
            ],
            compiler_params=pltpu.CompilerParams(collective_id=0, has_side_effects=True),
        )(jnp.swapaxes(walkers, 1, 2), cholesky, fields, weights, counts)
        return jnp.swapaxes(routed, 1, 2), comb

    in_specs = (P("walk", None, None), P("chol", None, None), P("walk", "chol"), P("walk"), P("walk"))
    return jax.shard_map(
        on_device, mesh=mesh, in_specs=in_specs, out_specs=(P("walk", None, None), P("walk")), check_vma=False
    )
```

```python
import functools

import jax
import jax.numpy as jnp
from jax import lax
from jax.experimental import pallas as pl
from jax.experimental.pallas import tpu as pltpu
from jax.sharding import PartitionSpec as P

F32 = jnp.float32
BF16 = jnp.bfloat16
MESH = pl.DeviceIdType.MESH
TAYLOR = 3
LANES = 128
ROOT_DT = 0.1


def split(a):
    high = a.astype(BF16)
    return high, (a - high.astype(F32)).astype(BF16)


def dot(a, b):
    return jnp.dot(a, b, preferred_element_type=F32)


def dot3(a, b):
    return dot(a[0], b[0]) + (dot(a[1], b[0]) + dot(a[0], b[1]))


def block_form(c):
    re, im = c[:, :LANES], c[:, LANES:]
    return jnp.concatenate([c, jnp.concatenate([-im, re], axis=1)], axis=0)


def kernel(
    nwalk, nchol, nelec,
    walk_hbm, chol_hbm, fields_s, weights_s, counts_s,
    out_ref, comb_s,
    wbuf, padt, top, lrows, pall, phi, plo, msgs, acomp, abuf, q0, q1, q2, cnew, pcand, qf, ring, tally,
    c_sem, l_send, l_recv, z_send, z_recv, f_send, f_recv, m_send, m_recv,
    a_send, a_recv, s_send, s_recv, g_send, g_recv, o_send, o_recv, r_send, r_recv, t_send, t_recv, n_send, n_recv,
):
    w = lax.axis_index("walk")
    me = lax.axis_index("chol")
    core = lax.rem(w, 2)
    chip = lax.div(w, 2)
    nchip = nwalk // 2
    partner = w + 1 - 2 * core
    walks, norb = wbuf.shape[0], wbuf.shape[2]
    rows = norb // nchol
    depth = top.shape[1]
    half = rows // 2
    side = 4
    gx, gy = lax.rem(me, side), lax.div(me, side)
    parity = lax.rem(chip, 2)
    band = rows * side
    mine_walker, mine_half = lax.div(gy, 2), lax.rem(gy, 2)
    first = -(-nelec // 16) * 8
    quarter = LANES // 2

    def walk_id(shift):
        return {"walk": lax.rem(w + nwalk + shift, nwalk)}

    def chip_id(shift, which):
        return {"walk": 2 * lax.rem(chip + nchip + shift, nchip) + which}

    def block(owner):
        at = lax.rem(owner, side) * side + lax.div(owner, side)
        return pl.ds(pl.multiple_of(at * rows, rows), rows)

    def at_band(bx):
        return pl.ds(pl.multiple_of(bx * band, band), band)

    def chip_at(dx, dy):
        return lax.rem(gy + side + dy, side) * side + lax.rem(gx + side + dx, side)

    def remote(src, dst, send, recv, device):
        return pltpu.make_async_remote_copy(
            src_ref=src, dst_ref=dst, send_sem=send, recv_sem=recv,
            device_id=device, device_id_type=MESH,
        )

    mine = block(me)
    copy_walk = pltpu.make_async_copy(walk_hbm, wbuf, c_sem.at[0])
    copy_top = pltpu.make_async_copy(chol_hbm.at[:, pl.ds(0, depth)], top, c_sem.at[1])
    copy_own = pltpu.make_async_copy(chol_hbm.at[:, mine], lrows.at[me], c_sem.at[2])
    copy_walk.start()
    copy_top.start()
    copy_own.start()

    barrier = pltpu.get_barrier_semaphore()

    @pl.loop(1, nchol)
    def _(k):
        pl.semaphore_signal(barrier, inc=1, device_id={"chol": lax.rem(me + k, nchol)}, device_id_type=MESH)

    greet = [{"walk": partner}]
    for shift in (1, -1):
        greet += [chip_id(shift, core), chip_id(shift, 1 - core)]
    for shift in (3, -3, 4, -4):
        greet.append(chip_id(shift, core))
    for device in greet:
        pl.semaphore_signal(barrier, inc=1, device_id=device, device_id_type=MESH)
    pl.semaphore_wait(barrier, nchol - 1 + len(greet))

    def piece(owner, which, part):
        return lrows.at[owner, which, pl.ds(pl.multiple_of(part * half, 8), half)]

    def l_copy(k, owner, target):
        return remote(chol_hbm.at[core, pl.ds(pl.multiple_of(
            (lax.rem(target, side) * side + lax.div(target, side)) * rows + parity * half, 8), half)],
                      piece(owner, core, parity), l_send.at[k], l_recv.at[k], {"chol": target})

    def z_copy(k, owner, part):
        return remote(piece(owner, core, part), piece(owner, core, part), z_send.at[k], z_recv.at[k],
                      chip_id(2 * lax.rem(owner, 2) - 1, core))

    def f_copy(k, owner, which, part, slot):
        return remote(piece(owner, which, part), piece(owner, which, part),
                      f_send.at[slot, k], f_recv.at[slot, k], {"walk": partner})

    @pl.loop(1, nchol)
    def _(k):
        l_copy(k, me, lax.rem(me + k, nchol)).start()

    here = nchip // 2

    def spread(buf, send, recv, stage):
        if stage == 0:
            own = buf.at[here, core]
            return [remote(own, own, send.at[0], recv.at[0], {"walk": partner})] + [
                remote(own, buf.at[here - d, core], send.at[j], recv.at[j], chip_id(d, c))
                for j, d, c in ((1, 1, core), (2, 1, 1 - core), (3, -1, core), (4, -1, 1 - core))]
        if stage == 1:
            return [remote(buf.at[here - 1:here + 2], buf.at[here - d - 1:here - d + 2],
                           send.at[j], recv.at[j], chip_id(d, core)) for j, d in ((5, 3), (6, -3))]
        return [remote(buf.at[here - 4:here], buf.at[here - 8:here - 4], send.at[7], recv.at[7], chip_id(4, core)),
                remote(buf.at[here + 1:here + 4], buf.at[here + 5:here + 8], send.at[8], recv.at[8], chip_id(-4, core))]

    weights_run, counts_run = (ring, r_send, r_recv), (tally, t_send, t_recv)

    def spread_start(run, stage):
        for copy in spread(*run, stage):
            copy.start()

    def spread_wait(run, stage):
        for copy in spread(*run, stage):
            copy.wait()

    for i in range(walks):
        tally[here, core, i:i + 1, :] = jnp.full((1, LANES), counts_s[i].astype(F32))
    spread_start(counts_run, 0)

    copy_walk.wait()
    for i in range(walks):
        padt[i, :, 96:LANES, :] = jnp.zeros((2, LANES - 96, norb), F32)
        padt[i, 0, 0:nelec, :] = wbuf[i, 0:nelec, :]
        padt[i, 1, 0:nelec, :] = wbuf[i, nelec:2 * nelec, :]
    for i in range(walks):
        pall[i] = padt[i].reshape(2 * LANES, norb).T
        high, low = split(pall[i])
        phi[i] = high
        plo[i] = low

    copy_top.wait()
    top_split = split(top[...].reshape(walks * depth, norb))
    at_row = lax.broadcasted_iota(jnp.int32, (LANES, LANES), 0)
    at_col = lax.broadcasted_iota(jnp.int32, (LANES, LANES), 1)
    unit = jnp.where((at_row == at_col) & (at_row < nelec), 1.0, 0.0).astype(F32)
    unit_row = jnp.concatenate([unit, jnp.zeros_like(unit)], axis=1)
    inside = lax.broadcasted_iota(jnp.int32, (LANES, 2 * LANES), 0) < nelec

    stage = []
    for i in range(walks):
        moment = dot3(top_split, (phi[i], plo[i]))
        err = jnp.where(inside, unit_row - pall[i, 0:LANES, :], 0.0)
        stage.append((moment, err))
    later = []
    for moment, err in stage:
        left = jnp.concatenate([err, moment], axis=0)
        prod = dot3(split(left), split(block_form(err)))
        later.append((prod[:LANES], moment + prod[LANES:]))
    for i, (err2, moment) in enumerate(later):
        left = jnp.concatenate([err2, moment], axis=0)
        prod = dot3(split(left), split(block_form(err2)))
        err4 = prod[:LANES]
        moment = moment + prod[LANES:]
        tr = (unit + err4[:, :LANES]).T[:depth]
        ti = err4[:, LANES:].T[:depth]
        log_part = jnp.zeros((1, 1), F32)
        for g in range(2):
            mr = moment[g * depth:(g + 1) * depth, :LANES]
            mi = moment[g * depth:(g + 1) * depth, LANES:]
            xr = ROOT_DT * jnp.sum(mr * tr - mi * ti, keepdims=True)
            xi = ROOT_DT * jnp.sum(mr * ti + mi * tr, keepdims=True)
            field = fields_s[i, g]
            log_part = log_part + (field * xr - 0.5 * (xr * xr - xi * xi))
            at = 2 * i + g
            msgs[0, me, at:at + 1, :] = jnp.broadcast_to(ROOT_DT * xi, (1, LANES))
            msgs[0, me, 4 + at:5 + at, :] = jnp.broadcast_to(ROOT_DT * (field - xr), (1, LANES))
        msgs[0, me, 8 + i:9 + i, :] = jnp.broadcast_to(log_part, (1, LANES))

    spread_wait(counts_run, 0)
    spread_start(counts_run, 1)

    def m_copy(k, owner, target):
        return remote(msgs.at[0, owner], msgs.at[0, owner], m_send.at[k], m_recv.at[k], {"chol": target})

    @pl.loop(1, nchol)
    def _(k):
        m_copy(k, me, lax.rem(me + k, nchol)).start()

    @pl.loop(1, nchol)
    def _(k):
        owner = lax.rem(me + nchol - k, nchol)
        l_copy(k, owner, owner).wait_recv()
        z_copy(k, owner, parity).start()
        f_copy(k, owner, core, parity, 0).start()

    @pl.loop(1, nchol)
    def _(k):
        owner = lax.rem(me + nchol - k, nchol)
        m_copy(k, owner, owner).wait_recv()

    cols = pl.multiple_of(mine_half * first, 8)

    def n_copy(j, shift):
        return remote(msgs.at[0, :, pl.ds(0, 8)], msgs.at[j + 1, :, pl.ds(0, 8)], n_send.at[j], n_recv.at[j], walk_id(shift))

    def p_copy(j, shift):
        return remote(padt.at[:, :, pl.ds(cols, quarter)], pcand.at[j], n_send.at[2 + j], n_recv.at[2 + j], walk_id(shift))

    n_copy(0, 1).start()
    n_copy(1, -1).start()
    spread_wait(counts_run, 1)
    spread_start(counts_run, 2)

    @pl.loop(1, nchol)
    def _(k):
        owner = lax.rem(me + nchol - k, nchol)
        z_copy(k, owner, 1 - parity).wait_recv()
        f_copy(k, owner, core, 1 - parity, 1).start()

    p_copy(0, 1).start()
    p_copy(1, -1).start()

    for i in range(walks):
        log_weight = msgs[0, 0, 8 + i:9 + i, :]
        for o in range(1, nchol):
            log_weight = log_weight + msgs[0, o, 8 + i:9 + i, :]
        ring[here, core, i:i + 1, :] = weights_s[i] * jnp.exp(log_weight)

    spread_start(weights_run, 0)

    @pl.loop(1, nchol)
    def _(k):
        owner = lax.rem(me + nchol - k, nchol)
        f_copy(k, owner, 1 - core, parity, 0).wait_recv()
        f_copy(k, owner, 1 - core, 1 - parity, 1).wait_recv()

    spread_wait(counts_run, 2)
    zero = jnp.zeros((1, LANES), F32)
    base_count = zero
    for d in range(-here, here):
        if d == 0:
            earlier = [core == 1, core < 0]
        elif d < 0:
            earlier = [chip + d >= 0] * 2
        else:
            earlier = [chip + d >= nchip] * 2
        for c in range(2):
            base_count = base_count + jnp.where(
                earlier[c], tally[here + d, c, 0:1, :] + tally[here + d, c, 1:2, :], 0.0)
    def counts_of(when_even, when_odd, i):
        return jnp.where(core == 0, tally[when_even[0], when_even[1], i:i + 1, :],
                         tally[when_odd[0], when_odd[1], i:i + 1, :])

    own_counts = [tally[here, core, i:i + 1, :] for i in range(walks)]
    left_counts = [counts_of((here - 1, 1), (here, 0), i) for i in range(walks)]
    right_counts = [counts_of((here, 1), (here + 1, 0), i) for i in range(walks)]
    left_start = base_count - left_counts[0] - left_counts[1]
    right_start = base_count + own_counts[0] + own_counts[1]
    weights_of = []
    for start, cs, valid in (
        (base_count, own_counts, w >= 0),
        (left_start, left_counts, w > 0),
        (right_start, right_counts, w < nwalk - 1),
    ):
        for i in range(walks):
            end = start + cs[i]
            picks = []
            for m in range(walks):
                target = jnp.full((1, LANES), (w * walks + m).astype(F32))
                hit = jnp.where(start <= target, 1.0, 0.0) * jnp.where(target < end, 1.0, 0.0)
                picks.append(jnp.where(valid, hit, 0.0))
            weights_of.append(picks)
            start = end
    n_copy(0, 1).wait_recv()
    n_copy(1, -1).wait_recv()
    for ri in range(2):
        for m in range(walks):
            for g in range(2):
                acc = jnp.zeros((nchol, LANES), F32)
                for j in range(3 * walks):
                    acc = acc + weights_of[j][m] * msgs[j // walks, :, 4 * ri + 2 * (j % walks) + g, :]
                cnew[4 * ri + 2 * m + g] = acc

    copy_own.wait()

    part = rows // 2
    pieces = []
    for h in range(2):
        sums = [jnp.zeros((part, norb), F32) for _ in range(4)]
        for o in range(nchol):
            for g in range(2):
                l = lrows[o, g, h * part:(h + 1) * part, :]
                for i in range(walks):
                    for ri in range(2):
                        at = 4 * ri + 2 * i + g
                        c = jnp.concatenate([cnew[at, o:o + 1, :]] * (norb // LANES), axis=1)
                        sums[2 * i + ri] = sums[2 * i + ri] + c * l
        pieces.append(sums)
    for i in range(walks):
        for ri in range(2):
            for h in range(2):
                acomp[i, ri, h * part:(h + 1) * part, :] = pieces[h][2 * i + ri]

    def band_rows(by):
        return pl.ds(pl.multiple_of(by * rows, rows), rows)

    def a_copy(d):
        to = lax.rem(gy + d, side)
        return remote(acomp.at[lax.div(to, 2)], abuf.at[:, band_rows(gy)], a_send.at[d], a_recv.at[d],
                      {"chol": chip_at(0, d)})

    for d in (2, 1, 3):
        a_copy(d).start()
    abuf[:, band_rows(gy), :] = acomp[mine_walker]
    p_copy(0, 1).wait_recv()
    p_copy(1, -1).wait_recv()
    picked = jnp.zeros((2, quarter, norb), F32)
    for j in range(3 * walks):
        i = j % walks
        source = padt[i, :, pl.ds(cols, quarter), :] if j < walks else pcand[j // walks - 1, i]
        pick = jnp.where(mine_walker == 0, weights_of[j][0], weights_of[j][1])
        picked = picked + jnp.concatenate([pick] * (norb // LANES), axis=1)[None] * source
    q0[...] = picked.reshape(2 * quarter, norb).T
    spread_wait(weights_run, 0)
    spread_start(weights_run, 1)
    q_split = split(q0[...])
    minus = jnp.where(lax.broadcasted_iota(jnp.int32, (band, LANES), 1) < quarter, -1.0, 1.0).astype(F32)

    def apply(oper, values, depth_of):
        prod = dot3(oper, values)
        return prod[:depth_of] + minus[:depth_of] * pltpu.roll(prod[depth_of:], quarter, 1)

    def strip(by):
        return pl.ds(pl.multiple_of(gx * band + by * rows, rows), rows)

    def s_copy(e, d):
        ref = q1.at[strip(lax.rem(gy + side - e, side))]
        return remote(ref, ref, s_send.at[e, d], s_recv.at[e, d], {"chol": chip_at(d, 0)})

    for e in (0, 1, 3, 2):
        by = lax.rem(gy + side - e, side)
        if e:
            a_copy(e).wait_recv()
        q1[strip(by), :] = apply(split(abuf[:, band_rows(by), :].reshape(2 * rows, norb)), q_split, rows)
        for d in (2, 1, 3):
            s_copy(e, d).start()
    oper = split(abuf[...].reshape(2 * band, norb))

    def g_copy(n, q, d):
        ref = q.at[at_band(gx)]
        return remote(ref, ref, g_send.at[n, d], g_recv.at[n, d], {"chol": chip_at(d, 0)})

    series = q0[at_band(gx), :] + q1[at_band(gx), :]
    spread_wait(weights_run, 1)
    spread_start(weights_run, 2)
    for n in range(2, TAYLOR + 1):
        if n == 2:
            for e in (0, 1, 3, 2):
                for d in (1, 3, 2):
                    s_copy(e, d).wait_recv()
            term = apply(oper, split(q1[...]), band) / n
            q2[at_band(gx), :] = term
            for d in (2, 1, 3):
                g_copy(1, q2, d).start()
        else:
            for d in (1, 3, 2):
                g_copy(1, q2, d).wait_recv()
            term = apply(oper, split(q2[...]), band) / n
        series = series + term
    turned = series.T
    for c in range(2):
        qf[gy, c, :, at_band(gx)] = turned[c * quarter:c * quarter + first]

    def o_copy(c, sem, origin, to):
        (da, db), (ta, tb) = origin, to
        dx, dy = (da, db) if c == 0 else (db, da)
        tx, ty = (ta, tb) if c == 0 else (tb, ta)
        ref = qf.at[lax.rem(gy + side + dy, side), c, :,
                    pl.ds(pl.multiple_of(lax.rem(gx + side + dx, side) * band, band), band)]
        return remote(ref, ref, o_send.at[c, sem], o_recv.at[c, sem], {"chol": chip_at(tx, ty)})

    def o_send_first(c, d):
        return o_copy(c, d, (0, 0), (d, 0))

    def o_send_second(c, d, e):
        return o_copy(c, 4 * d + e, (-d, 0), (0, e)) if d else o_copy(c, 16 + e, (0, 0), (0, e))

    def o_recv_first(c, d):
        return o_copy(c, d, (-d, 0), (d, 0))

    def o_recv_second(c, d, e):
        return o_copy(c, 4 * d + e, (-d, -e), (0, e)) if d else o_copy(c, 16 + e, (0, -e), (0, e))

    for d in (2, 1, 3):
        for c in range(2):
            o_send_first(c, d).start()
    for d in (2, 1, 3):
        for c in range(2):
            o_send_second(c, 0, d).start()
    spread_wait(weights_run, 2)
    zero = jnp.zeros((1, LANES), F32)
    total, base = zero, zero
    for d in range(-here, here):
        if d == 0:
            earlier = [core == 1, core < 0]
        elif d < 0:
            earlier = [chip + d >= 0] * 2
        else:
            earlier = [chip + d >= nchip] * 2
        for c in range(2):
            pair = ring[here + d, c, 0:1, :] + ring[here + d, c, 1:2, :]
            total = total + pair
            base = base + jnp.where(earlier[c], pair, 0.0)
    running = base
    for i in range(walks):
        running = running + ring[here, core, i:i + 1, :]
        comb_s[i] = jnp.max(nwalk * walks * running / total)

    for d in (1, 3, 2):
        for c in range(2):
            o_recv_first(c, d).wait_recv()
            for e in (2, 1, 3):
                o_send_second(c, d, e).start()
    for c in range(2):
        for d in (0, 1, 3, 2):
            for e in (1, 3, 2):
                o_recv_second(c, d, e).wait_recv()
    rest = nelec - first
    for i in range(walks):
        for c in range(2):
            wbuf[i, c * nelec:c * nelec + first, :] = qf[2 * i, c]
            wbuf[i, c * nelec + first:(c + 1) * nelec, :] = qf[2 * i + 1, c, 0:rest, :]
        pltpu.make_async_copy(wbuf.at[i], out_ref.at[i], c_sem.at[3 + i]).start()

    @pl.loop(1, nchol)
    def _(k):
        owner = lax.rem(me + nchol - k, nchol)
        l_copy(k, owner, owner).wait_send()
        z_copy(k, owner, parity).wait_send()
        f_copy(k, owner, core, parity, 0).wait_send()
        f_copy(k, owner, core, 1 - parity, 1).wait_send()
        m_copy(k, owner, owner).wait_send()

    for copy in (n_copy, p_copy):
        copy(0, 1).wait_send()
        copy(1, -1).wait_send()
    for d in range(1, side):
        a_copy(d).wait_send()
        for e in range(side):
            s_copy(e, d).wait_send()
        g_copy(1, q2, d).wait_send()
        for c in range(2):
            o_send_first(c, d).wait_send()
            for e in range(side):
                o_send_second(c, e, d).wait_send()
    for i in range(walks):
        pltpu.make_async_copy(wbuf.at[i], out_ref.at[i], c_sem.at[3 + i]).wait()


def hand_over(values, marks, values_out, marks_out):
    values_out[...] = values[...]
    for i in range(marks.shape[0]):
        marks_out[i] = marks[i]


def solution(mesh):
    nwalk, nchol = mesh.shape["walk"], mesh.shape["chol"]

    def on_device(walkers, cholesky, fields, weights, counts):
        walks, norb, width = walkers.shape
        nelec = width // 2
        ng = cholesky.shape[0]
        rows = norb // nchol
        depth = -(-nelec // 8) * 8
        vmem = pltpu.VMEM
        dma = pltpu.SemaphoreType.DMA
        smem = pl.BlockSpec(memory_space=pltpu.SMEM)
        hbm = pl.BlockSpec(memory_space=pl.ANY)
        routed, comb = pl.pallas_call(
            functools.partial(kernel, nwalk, nchol, nelec),
            out_shape=(
                jax.ShapeDtypeStruct((walks, width, norb), F32),
                jax.ShapeDtypeStruct((walks,), F32),
            ),
            in_specs=[hbm, hbm, smem, smem, smem],
            out_specs=(hbm, smem),
            scratch_shapes=[
                vmem((walks, width, norb), F32),
                vmem((walks, 2, LANES, norb), F32),
                vmem((ng, depth, norb), F32),
                vmem((nchol, ng, rows, norb), F32),
                vmem((walks, norb, 2 * LANES), F32),
                vmem((walks, norb, 2 * LANES), BF16),
                vmem((walks, norb, 2 * LANES), BF16),
                vmem((3, nchol, 16, LANES), F32),
                vmem((walks, 2, rows, norb), F32),
                vmem((2, 4 * rows, norb), F32),
                vmem((norb, LANES), F32),
                vmem((norb, LANES), F32),
                vmem((norb, LANES), F32),
                vmem((8, nchol, LANES), F32),
                vmem((2, walks, 2, LANES // 2, norb), F32),
                vmem((4, 2, -(-nelec // 16) * 8, norb), F32),
                vmem((nwalk // 2, 2, 8, LANES), F32),
                vmem((nwalk // 2, 2, 8, LANES), F32),
                dma((5,)),
                dma((nchol,)), dma((nchol,)), dma((nchol,)), dma((nchol,)),
                dma((2, nchol)), dma((2, nchol)), dma((nchol,)), dma((nchol,)),
                dma((4,)), dma((4,)), dma((4, 4)), dma((4, 4)), dma((2, 4)), dma((2, 4)), dma((2, 20)), dma((2, 20)),
                dma((9,)), dma((9,)), dma((9,)), dma((9,)),
                dma((4,)), dma((4,)),
            ],
            compiler_params=pltpu.CompilerParams(collective_id=0, has_side_effects=True),
        )(jnp.swapaxes(walkers, 1, 2), cholesky, fields, weights, counts)
        whole = pl.BlockSpec(memory_space=pltpu.VMEM)
        routed, comb = pl.pallas_call(
            hand_over,
            out_shape=(jax.ShapeDtypeStruct(routed.shape, F32), jax.ShapeDtypeStruct(comb.shape, F32)),
            in_specs=[whole, smem],
            out_specs=(whole, smem),
        )(routed, comb)
        return jnp.swapaxes(routed, 1, 2), comb

    in_specs = (P("walk", None, None), P("chol", None, None), P("walk", "chol"), P("walk"), P("walk"))
    return jax.shard_map(
        on_device, mesh=mesh, in_specs=in_specs, out_specs=(P("walk", None, None), P("walk")), check_vma=False
    )
```
